32 devices in a mesh: tg: 8 (over y, x, core), ep: 4 (over z).
Axes of the slice: x: 2, y: 2, z: 4, core: 2. Of those that a mesh axis runs over, the one named last changes fastest.
Arguments:
- tokens: bfloat16 [16384, 384], P(('tg', 'ep')), may hold values from -6 to 6
- timesteps: int32 [64], replicated, may hold values from 0 to 999, as said below
- labels: int32 [64], replicated, may hold values from 0 to 999
- routes: int32 [16384, 2], P(('tg', 'ep')), may hold values from 0 to 15, as said below
- time_table: bfloat16 [1000, 384], replicated, may hold values from -4.1875 to 4.1875
- class_table: bfloat16 [1000, 384], replicated, may hold values from -4.1875 to 4.1875
- ada_weight: bfloat16 [384, 2304], replicated, may hold values from -0.3125 to 0.3125
- ada_bias: float32 [2304], replicated, may hold values from -3 to 3
- gain_attn: float32 [384], replicated, may hold values from 0.5 to 1.5
- gain_ffn: float32 [384], replicated, may hold values from 0.5 to 1.5
- qkv_weight: bfloat16 [384, 1152], replicated, may hold values from -0.3125 to 0.3125
- proj_weight: bfloat16 [384, 384], replicated, may hold values from -1.25 to 1.25
- router_weight: bfloat16 [384, 16], replicated, may hold values from -0.625 to 0.625
- shared_in: bfloat16 [384, 3072], replicated, may hold values from -0.3125 to 0.3125
- shared_out: bfloat16 [3072, 384], replicated, may hold values from -0.15625 to 0.15625
- expert_in: bfloat16 [16, 384, 1536], P('ep', None, 'tg'), may hold values from -0.3125 to 0.3125
- expert_out: bfloat16 [16, 1536, 384], P('ep', 'tg'), may hold values from -0.15625 to 0.15625
- grad_out: bfloat16 [16384, 384], P(('tg', 'ep')), may hold values from -6 to 6
Outputs:
- out: bfloat16 [16384, 384], P(('tg', 'ep'))
- grad_tokens: float32 [16384, 384], P(('tg', 'ep'))
- grad_time_table: float32 [1000, 384], replicated
- grad_class_table: float32 [1000, 384], replicated
- grad_ada_weight: float32 [384, 2304], replicated
- grad_ada_bias: float32 [2304], replicated
- grad_gain_attn: float32 [384], replicated
- grad_gain_ffn: float32 [384], replicated
- grad_qkv_weight: float32 [384, 1152], replicated
- grad_proj_weight: float32 [384, 384], replicated
- grad_router: float32 [384, 16], replicated
- grad_shared_in: float32 [384, 3072], replicated
- grad_shared_out: float32 [3072, 384], replicated
- grad_expert_in: float32 [16, 384, 1536], P('ep', None, 'tg')
- grad_expert_out: float32 [16, 1536, 384], P('ep', 'tg')
The draws below stay inside these ranges and needn't reach their ends.
Inputs may be any that keep to these rules, and one draw needn't show every extreme that they name: With G = 8 groups, the images g * 8 to (g + 1) * 8 - 1 have timesteps t with g * 1000 <= G * t < (g + 1) * 1000; the first image of each group has the smallest such t and the last image the largest. `routes`: each row names two different experts. In the rows of one device no expert is named by more than 256 rows. For each group of 2048 rows (one index of tg) one expert is named by exactly 256 rows on every device of the group.
All inputs are finite; a program needn't handle non-finite values.
Results may differ from the reference program's by a relative error of at most 0.015.
The reference program's roundings to bfloat16 on the way count: a program that leaves them out, or rounds other values in their place, can miss the bound.
Values may be sent and summed in bfloat16 or wider, within the bound.
No kernel may reach another device: no remote copies, remote signals or barrier semaphores. Data moves between devices by JAX's collectives and lax.ppermute only.
A program may use at most 192 MiB of HBM per device.

```python
import jax
import jax.numpy as jnp
from jax import lax

D = 384
HEADS = 6
HEAD_DIM = 64
FF = 1536
EXPERTS = 16
SHARED = 2
TSTEPS = 1000
CLASSES = 1000
PATCHES = 256
TOK_DEV = 512
IMG_GROUP = 8
IMAGES = 64
TOKENS = 16384


def draw_timesteps(key, part):
    groups = IMAGES // IMG_GROUP
    image_ids = jnp.arange(IMAGES, dtype=jnp.int32)
    image_group = image_ids // IMG_GROUP
    within = image_ids % IMG_GROUP
    lowest = (image_group * TSTEPS + groups - 1) // groups
    beyond = ((image_group + 1) * TSTEPS + groups - 1) // groups
    spread = beyond - lowest
    offset = jax.random.randint(key, (IMAGES,), 0, 1 << 20, dtype=jnp.int32) % spread
    offset = jnp.where(within == 0, 0, jnp.where(within == IMG_GROUP - 1, spread - 1, offset))
    return (lowest + offset).astype(jnp.int32)


def draw_routes(key, part):
    blocks = TOKENS // TOK_DEV
    groups = TOKENS // (IMG_GROUP * PATCHES)
    key_hot, key_pool, key_rank, key_pick, key_swap, key_step = jax.random.split(key, 6)
    hot_of_group = jax.random.randint(key_hot, (groups,), 0, EXPERTS, dtype=jnp.int32)
    group_of_block = jnp.arange(blocks, dtype=jnp.int32) // (blocks // groups)
    hot_expert = hot_of_group[group_of_block]
    expert_ids = jnp.arange(EXPERTS, dtype=jnp.int32)
    pool_score = jax.random.randint(key_pool, (blocks, EXPERTS), 0, 1 << 20, dtype=jnp.int32) * EXPERTS + expert_ids[None, :]
    pool_score = jnp.where(expert_ids[None, :] == hot_expert[:, None], jnp.int32(1 << 30), pool_score)
    others = jnp.argsort(pool_score, axis=1)[:, :EXPERTS - 1].astype(jnp.int32)
    row_ids = jnp.arange(TOK_DEV, dtype=jnp.int32)
    rank_score = jax.random.randint(key_rank, (blocks, TOK_DEV), 0, 1 << 12, dtype=jnp.int32) * TOK_DEV + row_ids[None, :]
    row_rank = jnp.argsort(jnp.argsort(rank_score, axis=1), axis=1).astype(jnp.int32)
    hot_row = row_rank < TOK_DEV // 2
    pick_value = jax.random.randint(key_pick, (blocks, TOK_DEV), 0, 4096, dtype=jnp.int32)
    squared = pick_value * pick_value
    pool_size = jnp.where(hot_row, 7, 8)
    pick_index = pool_size * squared // (4096 * 4096)
    step_value = jax.random.randint(key_step, (blocks, TOK_DEV), 1, 8, dtype=jnp.int32)
    partner_slot = pick_index
    cold_first_slot = 7 + pick_index
    cold_second_slot = 7 + (pick_index + step_value) % 8
    partner = jnp.take_along_axis(others, partner_slot, axis=1)
    cold_first = jnp.take_along_axis(others, cold_first_slot, axis=1)
    cold_second = jnp.take_along_axis(others, cold_second_slot, axis=1)
    first_pick = jnp.where(hot_row, hot_expert[:, None], cold_first)
    second_pick = jnp.where(hot_row, partner, cold_second)
    swapped = jax.random.randint(key_swap, (blocks, TOK_DEV), 0, 2, dtype=jnp.int32) == 1
    former = jnp.where(swapped, second_pick, first_pick)
    latter = jnp.where(swapped, first_pick, second_pick)
    return jnp.stack([former, latter], axis=-1).reshape(TOKENS, 2).astype(jnp.int32)


def place_ends(array, stream_key, smallest, high):
    longest = array.shape.index(max(array.shape))
    spots = []
    for shift in (0, 1):
        where = [jax.random.randint(jax.random.fold_in(stream_key, axis), (), 0, length) for axis, length in enumerate(array.shape)]
        where[longest] = (where[longest] + shift) % array.shape[longest]
        spots.append(tuple(where))
    return array.at[spots[0]].set(smallest).at[spots[1]].set(high)


def level_of(stream_key, extent, cuts, least, largest):
    factor_of = 1.0
    for dim, blocks in cuts:
        draws = jax.random.uniform(jax.random.fold_in(jax.random.fold_in(stream_key, 6), dim), (blocks,), jnp.float32, least / len(cuts), largest / len(cuts))
        factor_of = factor_of * jnp.repeat(jnp.exp(draws), extent[dim] // blocks).reshape((-1,) + (1,) * (len(extent) - 1 - dim))
    return factor_of


def gaussian(stream_key, shape, width, most, cuts=(), held_as=jnp.bfloat16):
    drawn = width * jax.random.normal(stream_key, shape, jnp.float32)
    if cuts:
        drawn = drawn * level_of(stream_key, shape, cuts, -0.22, 0.18)
    return jnp.clip(drawn, -most, most).astype(held_as)


def setup_inputs(seed: int = 0) -> dict:
    splits = jax.random.split(jax.random.key(seed), 19)
    return {
        "tokens": gaussian(splits[0], (TOKENS, D), 1.0, 6.0, ((0, 32),)),
        "timesteps": draw_timesteps(jax.random.fold_in(splits[18], 71), 0),
        "labels": place_ends(jax.random.randint(splits[2], (IMAGES,), 0, CLASSES), jax.random.fold_in(splits[2], 1), 0, CLASSES - 1).astype(jnp.int32),
        "routes": draw_routes(jax.random.fold_in(splits[18], 71), 0),
        "time_table": gaussian(splits[4], (TSTEPS, D), 0.7, 4.1875),
        "class_table": gaussian(splits[5], (CLASSES, D), 0.7, 4.1875),
        "ada_weight": gaussian(splits[6], (D, 6 * D), D ** -0.5, 0.3125),
        "ada_bias": gaussian(splits[7], (6 * D,), 0.5, 3.0, (), jnp.float32),
        "gain_attn": jnp.clip(1.0 + 0.1 * jax.random.normal(splits[8], (D,), jnp.float32), 0.5, 1.5),
        "gain_ffn": jnp.clip(1.0 + 0.1 * jax.random.normal(splits[9], (D,), jnp.float32), 0.5, 1.5),
        "qkv_weight": gaussian(splits[10], (D, 3 * D), D ** -0.5, 0.3125),
        "proj_weight": gaussian(splits[11], (D, D), (D // 16) ** -0.5, 1.25),
        "router_weight": gaussian(splits[12], (D, EXPERTS), (D // 4) ** -0.5, 0.625),
        "shared_in": gaussian(splits[13], (D, SHARED * FF), D ** -0.5, 0.3125),
        "shared_out": gaussian(splits[14], (SHARED * FF, D), FF ** -0.5, 0.15625),
        "expert_in": gaussian(splits[15], (EXPERTS, D, FF), D ** -0.5, 0.3125, ((0, 4), (2, 8))),
        "expert_out": gaussian(splits[16], (EXPERTS, FF, D), FF ** -0.5, 0.15625, ((0, 4), (1, 8))),
        "grad_out": gaussian(splits[17], (TOKENS, D), 1.0, 6.0, ((0, 32),)),
    }


@jax.custom_vjp
def low(v):
    return lax.optimization_barrier(v.astype(jnp.bfloat16)).astype(jnp.float32)

@jax.custom_vjp
def low_back(v):
    return v

def low_keep(v):
    return (low(v), None)

def low_pass(kept, grad):
    return (grad,)

def back_keep(v):
    return (v, None)

def back_low(kept, grad):
    return (low(grad),)
low.defvjp(low_keep, low_pass)
low_back.defvjp(back_keep, back_low)

def product(left, right):
    return jnp.dot(left, right, precision=lax.Precision.HIGHEST)

def normalize(values):
    centred = values - lax.optimization_barrier(jnp.mean(values, axis=-1, keepdims=True))
    return centred * lax.rsqrt(lax.optimization_barrier(jnp.mean(centred * centred, axis=-1, keepdims=True)) + 1e-06)

def softmax_rows(scores):
    shifted = jnp.exp(scores - lax.optimization_barrier(jnp.max(scores, axis=-1, keepdims=True)))
    return shifted / lax.optimization_barrier(jnp.sum(shifted, axis=-1, keepdims=True))

def attend_block(qkv_block):
    block_count = qkv_block.shape[0]
    head_shape = (block_count, PATCHES, HEADS, HEAD_DIM)
    queries = qkv_block[..., :D].reshape(head_shape)
    key_rows = qkv_block[..., D:2 * D].reshape(head_shape)
    value_rows = qkv_block[..., 2 * D:].reshape(head_shape)
    raw_scores = jnp.einsum('bqhd,bkhd->bhqk', queries, key_rows, precision=lax.Precision.HIGHEST)
    scores = low_back(raw_scores * HEAD_DIM ** (-0.5))
    probability = low(softmax_rows(scores))
    mixed_rows = jnp.einsum('bhqk,bkhd->bqhd', probability, value_rows, precision=lax.Precision.HIGHEST)
    return low(low_back(mixed_rows.reshape(block_count, PATCHES, D)))

def expert_apply(rows, weight_in, weight_out):
    hidden = low_back(product(rows, weight_in))
    active = low(jax.nn.gelu(hidden, approximate=True))
    return low(low_back(product(active, weight_out)))

def forward(tokens, time_table, class_table, ada_weight, ada_bias, gain_attn, gain_ffn, qkv_weight, proj_weight, router_weight, shared_in, shared_out, expert_in, expert_out, timesteps, labels, routes):
    images = tokens.shape[0] // PATCHES
    condition = time_table[timesteps] + class_table[labels]
    modulation = (product(low(jax.nn.silu(condition)), ada_weight) + ada_bias).reshape(images, 6, 1, D)
    residual = tokens.reshape(images, PATCHES, D)
    normed = low(normalize(residual) * gain_attn * (1.0 + modulation[:, 1]) + modulation[:, 0])
    qkv_rows = low(low_back(product(normed.reshape(-1, D), qkv_weight)))
    blocks = qkv_rows.reshape(images // 16, 16, PATCHES, 3 * D)
    mixed_rows = lax.map(jax.checkpoint(attend_block), blocks).reshape(-1, D)
    attn_out = low_back(product(mixed_rows, proj_weight)).reshape(images, PATCHES, D)
    middle = residual + modulation[:, 2] * attn_out
    normed_ffn = low(normalize(middle) * gain_ffn * (1.0 + modulation[:, 4]) + modulation[:, 3]).reshape(-1, D)
    router_probs = softmax_rows(product(normed_ffn, router_weight))
    chosen = jnp.take_along_axis(router_probs, routes, axis=1)
    gate_values = chosen / lax.optimization_barrier(jnp.sum(chosen, axis=1, keepdims=True))
    shared_hidden = low_back(product(normed_ffn, shared_in))
    shared_term = low_back(product(low(jax.nn.gelu(shared_hidden, approximate=True)), shared_out))
    row_limit = normed_ffn.shape[0] // 2

    def one_expert(running, packed):
        number, weight_in, weight_out = packed
        matches = routes == number
        hit_key = jnp.where(jnp.any(matches, axis=1), 0, 1).astype(jnp.int32)
        row_order = jnp.argsort(hit_key, stable=True)[:row_limit]
        weight = lax.optimization_barrier(jnp.sum(jnp.where(matches, gate_values, 0.0), axis=1))[row_order]
        result = expert_apply(low_back(normed_ffn[row_order]), weight_in, weight_out)
        return (running.at[row_order].add(weight[:, None] * result), None)
    routed, unused = lax.scan(jax.checkpoint(one_expert), jnp.zeros_like(normed_ffn), (jnp.arange(EXPERTS, dtype=jnp.int32), expert_in, expert_out))
    ffn_out = (routed + shared_term).reshape(images, PATCHES, D)
    return (middle + modulation[:, 5] * ffn_out).reshape(-1, D)

def reference(tokens, timesteps, labels, routes, time_table, class_table, ada_weight, ada_bias, gain_attn, gain_ffn, qkv_weight, proj_weight, router_weight, shared_in, shared_out, expert_in, expert_out, grad_out):
    floats = [item.astype(jnp.float32) for item in (tokens, time_table, class_table, ada_weight, ada_bias, gain_attn, gain_ffn, qkv_weight, proj_weight, router_weight, shared_in, shared_out, expert_in, expert_out)]

    def wrapped(*params):
        return forward(*params, timesteps, labels, routes)
    output, pullback = jax.vjp(wrapped, *floats)
    gradients = pullback(grad_out.astype(jnp.float32))
    return (output.astype(jnp.bfloat16), gradients[0], gradients[1], gradients[2], gradients[3], gradients[4], gradients[5], gradients[6], gradients[7], gradients[8], gradients[9], gradients[10], gradients[11], gradients[12], gradients[13])
```

```python
import jax
import jax.numpy as jnp
from jax import lax
from jax.experimental import pallas as pl
from jax.experimental.pallas import tpu as pltpu
from jax.sharding import PartitionSpec as P

HEAD_DIM = 64
PATCHES = 256
ROWS = 256
GELU_SCALE = 0.7978845608028654
GELU_CUBE = 0.044715


def normalize(values):
    centred = values - jnp.mean(values, axis=-1, keepdims=True)
    inverse = lax.rsqrt(jnp.mean(centred * centred, axis=-1, keepdims=True) + 1e-06)
    return (centred * inverse, inverse)


def norm_back(grad_normed, normed, inverse):
    mean_grad = jnp.mean(grad_normed, axis=-1, keepdims=True)
    mean_cross = jnp.mean(grad_normed * normed, axis=-1, keepdims=True)
    return inverse * (grad_normed - mean_grad - normed * mean_cross)


def gelu_tanh(values):
    return jax.nn.gelu(values, approximate=True)


def gelu_back(values, grad_values):
    return jax.vjp(gelu_tanh, values)[1](grad_values)[0]


def contract(left, right, left_dim, right_dim):
    return lax.dot_general(
        left, right, (((left_dim,), (right_dim,)), ((), ())), preferred_element_type=jnp.float32
    )


def expert_kernel(
    count_ref,
    rows_ref,
    grads_ref,
    place_row_ref,
    gate_row_ref,
    place_ref,
    in_ref,
    out_ref,
    routed_ref,
    grad_rows_ref,
    grad_gate_ref,
    grad_in_ref,
    grad_out_ref,
    column_ref,
    total_in_ref,
    total_out_ref,
):
    expert, block = pl.program_id(0), pl.program_id(1)
    tokens = rows_ref.shape[0]

    @pl.when((expert == 0) & (block == 0))
    def _():
        routed_ref[...] = jnp.zeros_like(routed_ref)
        grad_rows_ref[...] = jnp.zeros_like(grad_rows_ref)

    @pl.when(block == 0)
    def _():
        lanes = lax.broadcasted_iota(jnp.int32, place_ref.shape, 1)
        column = jnp.sum(jnp.where(lanes == expert, place_ref[...], 0.0), axis=1, keepdims=True)
        column_ref[...] = jnp.broadcast_to(column, column_ref.shape)
        total_in_ref[...] = jnp.zeros_like(total_in_ref)
        total_out_ref[...] = jnp.zeros_like(total_out_ref)
        grad_gate_ref[...] = jnp.zeros_like(grad_gate_ref)

    @pl.when(block * ROWS < count_ref[expert])
    def _():
        base = (block * ROWS).astype(jnp.float32)
        row_ids = lax.broadcasted_iota(jnp.int32, (ROWS, tokens), 0).astype(jnp.float32) + base
        hit = row_ids == place_row_ref[0]
        pick = jnp.where(hit, 1.0, 0.0).astype(jnp.bfloat16)
        gate = jnp.sum(jnp.where(hit, gate_row_ref[0], 0.0), axis=1, keepdims=True)
        rows = contract(pick, rows_ref[...], 1, 0).astype(jnp.bfloat16)
        grads = contract(pick, grads_ref[...], 1, 0)
        hidden = contract(rows, in_ref[0], 1, 0)
        square = hidden * hidden
        bend = jnp.tanh(GELU_SCALE * hidden * (1.0 + GELU_CUBE * square))
        active = (0.5 * hidden * (1.0 + bend)).astype(jnp.bfloat16)
        slope = 0.5 * (1.0 + bend) + (0.5 * GELU_SCALE) * hidden * (1.0 - bend * bend) * (
            1.0 + (3.0 * GELU_CUBE) * square
        )
        produced = contract(active, out_ref[0], 1, 0).astype(jnp.bfloat16).astype(jnp.float32)
        grad_produced = (gate * grads).astype(jnp.bfloat16)
        grad_active = contract(grad_produced, out_ref[0], 1, 1)
        grad_hidden = (grad_active * slope).astype(jnp.bfloat16)
        total_in_ref[...] += contract(grad_hidden, rows, 0, 0)
        total_out_ref[...] += contract(active, grad_produced, 0, 0)
        grad_back = contract(grad_hidden, in_ref[0], 1, 1).astype(jnp.bfloat16)
        grad_gate = jnp.sum(grads * produced, axis=1, keepdims=True)
        grad_gate_ref[0] += jnp.sum(jnp.where(hit, grad_gate, 0.0), axis=0, keepdims=True)
        lane_ids = lax.broadcasted_iota(jnp.int32, (tokens, 128), 1).astype(jnp.float32) + base
        column = column_ref[...]
        place = jnp.concatenate(
            [
                jnp.where(column == lane_ids + float(start), 1.0, 0.0).astype(jnp.bfloat16)
                for start in range(0, ROWS, 128)
            ],
            axis=1,
        )
        routed_ref[...] += contract(place, (gate * produced).astype(jnp.bfloat16), 1, 0)
        grad_rows_ref[...] += contract(place, grad_back, 1, 0)

    @pl.when(block == pl.num_programs(1) - 1)
    def _():
        grad_in_ref[0] = total_in_ref[...].astype(jnp.bfloat16)
        grad_out_ref[0] = total_out_ref[...].astype(jnp.bfloat16)


def expert_stage(counts, rows, grads, place_rows, gate_rows, places, full_in, full_out):
    tokens, features = rows.shape
    experts, _, hidden = full_in.shape
    whole = lambda expert, block, counts: (0, 0)
    single = lambda expert, block, counts: (expert, 0, 0)
    row_spec = pl.BlockSpec((1, 1, tokens), single)
    weight_spec = pl.BlockSpec((1, hidden, features), single)
    token_spec = pl.BlockSpec((tokens, features), whole)
    return pl.pallas_call(
        expert_kernel,
        out_shape=(
            jax.ShapeDtypeStruct((tokens, features), jnp.float32),
            jax.ShapeDtypeStruct((tokens, features), jnp.float32),
            jax.ShapeDtypeStruct((experts, 1, tokens), jnp.float32),
            jax.ShapeDtypeStruct((experts, hidden, features), jnp.bfloat16),
            jax.ShapeDtypeStruct((experts, hidden, features), jnp.bfloat16),
        ),
        grid_spec=pltpu.PrefetchScalarGridSpec(
            num_scalar_prefetch=1,
            grid=(experts, tokens // 2 // ROWS),
            in_specs=[
                token_spec,
                token_spec,
                row_spec,
                row_spec,
                pl.BlockSpec((tokens, experts), whole),
                pl.BlockSpec((1, features, hidden), single),
                weight_spec,
            ],
            out_specs=[token_spec, token_spec, row_spec, weight_spec, weight_spec],
            scratch_shapes=[
                pltpu.VMEM((tokens, 128), jnp.float32),
                pltpu.VMEM((hidden, features), jnp.float32),
                pltpu.VMEM((hidden, features), jnp.float32),
            ],
        ),
        compiler_params=pltpu.CompilerParams(
            dimension_semantics=("arbitrary", "arbitrary"), vmem_limit_bytes=60 << 20
        ),
        name="expert_stage",
    )(counts, rows, grads, place_rows, gate_rows, places, full_in, full_out)


def place_tokens(routes, first_expert, experts):
    expert_ids = first_expert + jnp.arange(experts, dtype=jnp.int32)
    first_hit = (routes[:, 0:1] == expert_ids[None, :]).astype(jnp.float32)
    second_hit = (routes[:, 1:2] == expert_ids[None, :]).astype(jnp.float32)
    hits = first_hit + second_hit
    chunks = hits.reshape(-1, 256, experts)
    order = jnp.arange(256)
    earlier = (order[:, None] > order[None, :]).astype(jnp.bfloat16)
    within = jnp.einsum(
        "ij,cje->cie", earlier, chunks.astype(jnp.bfloat16), preferred_element_type=jnp.float32
    )
    chunk_totals = jnp.sum(chunks, axis=1)
    chunk_order = jnp.arange(chunks.shape[0])
    chunk_earlier = (chunk_order[:, None] > chunk_order[None, :]).astype(jnp.float32)
    offsets = jnp.sum(chunk_earlier[:, :, None] * chunk_totals[None, :, :], axis=1)
    places = jnp.where(chunks > 0.0, within + offsets[:, None, :], -1.0).reshape(-1, experts)
    counts = jnp.sum(chunk_totals, axis=0).astype(jnp.int32)
    return first_hit, second_hit, places, counts


def split_heads(qkv_block):
    block_count, patches, triple = qkv_block.shape
    features = triple // 3
    head_shape = (block_count, patches, features // HEAD_DIM, HEAD_DIM)
    return (
        qkv_block[..., :features].reshape(head_shape),
        qkv_block[..., features : 2 * features].reshape(head_shape),
        qkv_block[..., 2 * features :].reshape(head_shape),
    )


def attend_forward(qkv_block):
    queries, key_rows, value_rows = split_heads(qkv_block)
    score_scale = HEAD_DIM ** (-0.5)
    scores = (
        jnp.einsum("bqhd,bkhd->bhqk", queries, key_rows, preferred_element_type=jnp.float32)
        * score_scale
    )
    peak_value = jnp.max(scores, axis=-1, keepdims=True)
    shifted = jnp.exp(scores - peak_value)
    denominator = jnp.sum(shifted, axis=-1, keepdims=True)
    probability = (shifted / denominator).astype(jnp.bfloat16)
    mixed_rows = jnp.einsum(
        "bhqk,bkhd->bqhd", probability, value_rows, preferred_element_type=jnp.float32
    )
    mixed_rows = mixed_rows.reshape(qkv_block.shape[0], qkv_block.shape[1], -1).astype(jnp.bfloat16)
    return (mixed_rows, (peak_value + jnp.log(denominator))[..., 0])


def attend_backward(packed):
    qkv_block, grad_mixed, log_total = packed
    queries, key_rows, value_rows = split_heads(qkv_block)
    score_scale = HEAD_DIM ** (-0.5)
    scores = (
        jnp.einsum("bqhd,bkhd->bhqk", queries, key_rows, preferred_element_type=jnp.float32)
        * score_scale
    )
    probability = jnp.exp(scores - log_total[..., None])
    grad_heads = grad_mixed.reshape(queries.shape)
    grad_values = jnp.einsum(
        "bhqk,bqhd->bkhd",
        probability.astype(jnp.bfloat16),
        grad_heads,
        preferred_element_type=jnp.float32,
    )
    grad_probs = jnp.einsum(
        "bqhd,bkhd->bhqk", grad_heads, value_rows, preferred_element_type=jnp.float32
    )
    grad_scores = (
        probability * (grad_probs - jnp.sum(grad_probs * probability, axis=-1, keepdims=True))
    ).astype(jnp.bfloat16)
    grad_queries = (
        jnp.einsum("bhqk,bkhd->bqhd", grad_scores, key_rows, preferred_element_type=jnp.float32)
        * score_scale
    )
    grad_keys = (
        jnp.einsum("bhqk,bqhd->bkhd", grad_scores, queries, preferred_element_type=jnp.float32)
        * score_scale
    )
    merged = jnp.concatenate([grad_queries, grad_keys, grad_values], axis=2)
    return merged.reshape(qkv_block.shape[0], qkv_block.shape[1], -1).astype(jnp.bfloat16)


def shards(
    tokens,
    timesteps,
    labels,
    routes,
    time_table,
    class_table,
    ada_weight,
    ada_bias,
    gain_attn,
    gain_ffn,
    qkv_weight,
    proj_weight,
    router_weight,
    shared_in,
    shared_out,
    expert_in,
    expert_out,
    grad_out,
):
    count_tokens, features = tokens.shape
    images = count_tokens // PATCHES
    pair_count = images // 2
    ep_size = lax.axis_size("ep")
    experts = expert_in.shape[0]
    group = lax.axis_index("tg")
    device = group * ep_size + lax.axis_index("ep")
    routes_group = lax.all_gather(routes, "ep", axis=0, tiled=True)
    upstream_group = lax.all_gather(grad_out, "ep", axis=0, tiled=True)
    full_in = lax.all_gather(expert_in, "tg", axis=2, tiled=True)
    full_out = lax.all_gather(expert_out, "tg", axis=1, tiled=True)
    step_ids = jnp.arange(time_table.shape[0], dtype=jnp.int32)
    class_ids = jnp.arange(class_table.shape[0], dtype=jnp.int32)
    time_hot = (timesteps[:, None] == step_ids[None, :]).astype(jnp.bfloat16)
    class_hot = (labels[:, None] == class_ids[None, :]).astype(jnp.bfloat16)
    condition = jnp.dot(time_hot, time_table, preferred_element_type=jnp.float32) + jnp.dot(
        class_hot, class_table, preferred_element_type=jnp.float32
    )
    silu_low = jax.nn.silu(condition).astype(jnp.bfloat16)
    all_modulation = jnp.dot(silu_low, ada_weight, preferred_element_type=jnp.float32) + ada_bias
    modulation = lax.dynamic_slice_in_dim(all_modulation, device * images, images).reshape(
        images, 6, 1, features
    )
    group_gate = lax.dynamic_slice_in_dim(
        all_modulation[:, 5 * features :], group * images * ep_size, images * ep_size
    )
    grad_group = (
        (group_gate[:, None, :] * upstream_group.reshape(-1, PATCHES, features))
        .astype(jnp.bfloat16)
        .reshape(-1, features)
    )
    first_hit, second_hit, places, counts = place_tokens(
        routes_group, lax.axis_index("ep") * experts, experts
    )
    residual = tokens.astype(jnp.float32).reshape(images, PATCHES, features)
    normed_attn, inverse_attn = normalize(residual)
    factor_attn = 1.0 + modulation[:, 1]
    attn_in = (
        (normed_attn * gain_attn * factor_attn + modulation[:, 0])
        .astype(jnp.bfloat16)
        .reshape(-1, features)
    )
    qkv_rows = jnp.dot(attn_in, qkv_weight, preferred_element_type=jnp.float32).astype(jnp.bfloat16)
    qkv_blocks = qkv_rows.reshape(pair_count, 2, PATCHES, 3 * features)
    mixed_rows, log_total = lax.map(attend_forward, qkv_blocks)
    mixed_rows = mixed_rows.reshape(-1, features)
    attn_out = jnp.dot(mixed_rows, proj_weight, preferred_element_type=jnp.float32).reshape(
        images, PATCHES, features
    )
    middle = residual + modulation[:, 2] * attn_out
    normed_ffn, inverse_ffn = normalize(middle)
    factor_ffn = 1.0 + modulation[:, 4]
    ffn_in = (
        (normed_ffn * gain_ffn * factor_ffn + modulation[:, 3])
        .astype(jnp.bfloat16)
        .reshape(-1, features)
    )
    rows_group = lax.all_gather(ffn_in, "ep", axis=0, tiled=True)
    shared_hidden = jnp.dot(ffn_in, shared_in, preferred_element_type=jnp.float32)
    shared_active = gelu_tanh(shared_hidden).astype(jnp.bfloat16)
    shared_term = jnp.dot(shared_active, shared_out, preferred_element_type=jnp.float32)
    upstream = grad_out.astype(jnp.float32).reshape(images, PATCHES, features)
    grad_ffn = (modulation[:, 5] * upstream).reshape(-1, features)
    grad_shared_low = grad_ffn.astype(jnp.bfloat16)
    grad_shared_out = jnp.einsum(
        "rf,rd->fd", shared_active, grad_shared_low, preferred_element_type=jnp.float32
    )
    grad_shared_active = jnp.einsum(
        "rd,fd->rf", grad_shared_low, shared_out, preferred_element_type=jnp.float32
    )
    grad_shared_hidden = gelu_back(shared_hidden, grad_shared_active).astype(jnp.bfloat16)
    grad_shared_in = jnp.einsum(
        "rd,rf->df", ffn_in, grad_shared_hidden, preferred_element_type=jnp.float32
    )
    grad_ffn_in = jnp.einsum(
        "rf,df->rd", grad_shared_hidden, shared_in, preferred_element_type=jnp.float32
    )
    route_ids = jnp.arange(router_weight.shape[1], dtype=jnp.int32)
    first_hot = (routes_group[:, 0:1] == route_ids[None, :]).astype(jnp.float32)
    second_hot = (routes_group[:, 1:2] == route_ids[None, :]).astype(jnp.float32)
    logits = jnp.dot(rows_group, router_weight, preferred_element_type=jnp.float32)
    first_logit = jnp.sum(logits * first_hot, axis=1, keepdims=True)
    second_logit = jnp.sum(logits * second_hot, axis=1, keepdims=True)
    peak_logit = jnp.maximum(first_logit, second_logit)
    first_power = jnp.exp(first_logit - peak_logit)
    second_power = jnp.exp(second_logit - peak_logit)
    first_gate = first_power / (first_power + second_power)
    second_gate = second_power / (first_power + second_power)
    gates_here = first_hit * first_gate + second_hit * second_gate
    routed_part, grad_rows_part, grad_gates, grad_in_part, grad_out_part = expert_stage(
        counts,
        rows_group,
        grad_group,
        places.T[:, None, :],
        gates_here.T[:, None, :],
        places,
        full_in,
        full_out,
    )
    grad_hits = grad_gates[:, 0, :].T
    gate_pull = (
        first_gate
        * second_gate
        * jnp.sum(grad_hits * (first_hit - second_hit), axis=1, keepdims=True)
    )
    grad_logits = gate_pull * (first_hot - second_hot)
    grad_router = jnp.einsum(
        "rd,re->de",
        rows_group.astype(jnp.float32),
        grad_logits,
        precision=lax.Precision.HIGHEST,
    )
    grad_rows_part = grad_rows_part + jnp.einsum(
        "re,de->rd", grad_logits, router_weight.astype(jnp.float32), precision=lax.Precision.HIGHEST
    )
    grad_ffn_in = grad_ffn_in + lax.psum_scatter(
        grad_rows_part.astype(jnp.bfloat16), "ep", scatter_dimension=0, tiled=True
    ).astype(jnp.float32)
    routed = lax.psum_scatter(
        routed_part.astype(jnp.bfloat16), "ep", scatter_dimension=0, tiled=True
    ).astype(jnp.float32)
    ffn_out = (routed + shared_term).reshape(images, PATCHES, features)
    output = (middle + modulation[:, 5] * ffn_out).reshape(-1, features).astype(jnp.bfloat16)
    grad_gate_ffn = jnp.sum(upstream * ffn_out, axis=1)
    shard_in = (
        lax.psum_scatter(grad_in_part, "tg", scatter_dimension=1, tiled=True)
        .astype(jnp.float32)
        .transpose(0, 2, 1)
    )
    shard_out = lax.psum_scatter(grad_out_part, "tg", scatter_dimension=1, tiled=True).astype(
        jnp.float32
    )
    grad_ffn_cube = grad_ffn_in.reshape(images, PATCHES, features)
    grad_shift_ffn = jnp.sum(grad_ffn_cube, axis=1)
    cross_ffn = jnp.sum(grad_ffn_cube * normed_ffn, axis=1)
    grad_middle = upstream + norm_back(
        grad_ffn_cube * gain_ffn * factor_ffn, normed_ffn, inverse_ffn
    )
    grad_gate_attn = jnp.sum(grad_middle * attn_out, axis=1)
    grad_attn_low = (modulation[:, 2] * grad_middle).reshape(-1, features).astype(jnp.bfloat16)
    grad_proj = jnp.einsum(
        "rd,re->de", mixed_rows, grad_attn_low, preferred_element_type=jnp.float32
    )
    grad_mixed = jnp.einsum(
        "re,de->rd", grad_attn_low, proj_weight, preferred_element_type=jnp.float32
    ).astype(jnp.bfloat16)
    grad_qkv = lax.map(
        attend_backward,
        (qkv_blocks, grad_mixed.reshape(pair_count, 2, PATCHES, features), log_total),
    ).reshape(-1, 3 * features)
    grad_qkv_weight = jnp.einsum("rd,re->de", attn_in, grad_qkv, preferred_element_type=jnp.float32)
    grad_attn_in = jnp.einsum(
        "re,de->rd", grad_qkv, qkv_weight, preferred_element_type=jnp.float32
    ).reshape(images, PATCHES, features)
    grad_shift_attn = jnp.sum(grad_attn_in, axis=1)
    cross_attn = jnp.sum(grad_attn_in * normed_attn, axis=1)
    grad_tokens = grad_middle + norm_back(
        grad_attn_in * gain_attn * factor_attn, normed_attn, inverse_attn
    )
    image_sums = lax.all_gather(
        jnp.concatenate(
            [
                grad_shift_attn,
                cross_attn,
                grad_gate_attn,
                grad_shift_ffn,
                cross_ffn,
                grad_gate_ffn,
            ],
            axis=1,
        ),
        ("tg", "ep"),
        axis=0,
        tiled=True,
    ).reshape(-1, 6, features)
    all_pieces = all_modulation.reshape(-1, 6, features)
    grad_gain_attn = jnp.sum(image_sums[:, 1] * (1.0 + all_pieces[:, 1]), axis=0)
    grad_gain_ffn = jnp.sum(image_sums[:, 4] * (1.0 + all_pieces[:, 4]), axis=0)
    ones = jnp.ones_like(gain_attn)
    piece_gains = jnp.stack([ones, gain_attn, ones, ones, gain_ffn, ones])
    grad_modulation = (image_sums * piece_gains).reshape(-1, 6 * features)
    grad_ada_bias = jnp.sum(grad_modulation, axis=0)
    grad_ada_weight = jnp.einsum(
        "id,ie->de", silu_low.astype(jnp.float32), grad_modulation, precision=lax.Precision.HIGHEST
    )
    grad_silu = jnp.einsum(
        "ie,de->id",
        grad_modulation,
        ada_weight.astype(jnp.float32),
        precision=lax.Precision.HIGHEST,
    )
    grad_condition = jax.vjp(jax.nn.silu, condition)[1](grad_silu)[0]
    time_term = jnp.einsum(
        "is,id->sd", time_hot.astype(jnp.float32), grad_condition, precision=lax.Precision.HIGHEST
    )
    class_term = jnp.einsum(
        "ic,id->cd", class_hot.astype(jnp.float32), grad_condition, precision=lax.Precision.HIGHEST
    )
    low_sums = lax.psum(
        tuple(
            item.astype(jnp.bfloat16)
            for item in (grad_shared_in, grad_shared_out, grad_qkv_weight, grad_proj, grad_router)
        ),
        ("tg", "ep"),
    )
    shared_in_sum, shared_out_sum, qkv_sum, proj_sum, router_sum = (
        item.astype(jnp.float32) for item in low_sums
    )
    return (
        output,
        grad_tokens.reshape(-1, features),
        time_term,
        class_term,
        grad_ada_weight,
        grad_ada_bias,
        grad_gain_attn,
        grad_gain_ffn,
        qkv_sum,
        proj_sum,
        router_sum,
        shared_in_sum,
        shared_out_sum,
        shard_in,
        shard_out,
    )


def solution(mesh):
    in_specs = (
        P(("tg", "ep"), None),
        P(),
        P(),
        P(("tg", "ep"), None),
        P(),
        P(),
        P(),
        P(),
        P(),
        P(),
        P(),
        P(),
        P(),
        P(),
        P(),
        P("ep", None, "tg"),
        P("ep", "tg", None),
        P(("tg", "ep"), None),
    )
    out_specs = (
        P(("tg", "ep"), None),
        P(("tg", "ep"), None),
        P(),
        P(),
        P(),
        P(),
        P(),
        P(),
        P(),
        P(),
        P(),
        P(),
        P(),
        P("ep", None, "tg"),
        P("ep", "tg", None),
    )
    return jax.shard_map(shards, mesh=mesh, in_specs=in_specs, out_specs=out_specs, check_vma=False)
```

```python
import jax
import jax.numpy as jnp
from jax import lax
from jax.experimental import pallas as pl
from jax.experimental.pallas import tpu as pltpu
from jax.sharding import PartitionSpec as P

HEAD_DIM = 64
PATCHES = 256
ROWS = 256
GELU_SCALE = 0.7978845608028654
GELU_CUBE = 0.044715


def normalize(values):
    centred = values - jnp.mean(values, axis=-1, keepdims=True)
    inverse = lax.rsqrt(jnp.mean(centred * centred, axis=-1, keepdims=True) + 1e-06)
    return (centred * inverse, inverse)


def norm_back(grad_normed, normed, inverse):
    mean_grad = jnp.mean(grad_normed, axis=-1, keepdims=True)
    mean_cross = jnp.mean(grad_normed * normed, axis=-1, keepdims=True)
    return inverse * (grad_normed - mean_grad - normed * mean_cross)


def gelu_tanh(values):
    return jax.nn.gelu(values, approximate=True)


def gelu_back(values, grad_values):
    return jax.vjp(gelu_tanh, values)[1](grad_values)[0]


def contract(left, right, left_dim, right_dim):
    return lax.dot_general(
        left, right, (((left_dim,), (right_dim,)), ((), ())), preferred_element_type=jnp.float32
    )


def expert_kernel(
    count_ref,
    rows_ref,
    grads_ref,
    place_row_ref,
    gate_row_ref,
    place_ref,
    in_ref,
    out_ref,
    routed_ref,
    grad_rows_ref,
    grad_gate_ref,
    grad_in_ref,
    grad_out_ref,
    column_ref,
    total_in_ref,
    total_out_ref,
):
    expert, block = pl.program_id(0), pl.program_id(1)
    tokens = rows_ref.shape[0]

    @pl.when((expert == 0) & (block == 0))
    def _():
        routed_ref[...] = jnp.zeros_like(routed_ref)
        grad_rows_ref[...] = jnp.zeros_like(grad_rows_ref)

    @pl.when(block == 0)
    def _():
        lanes = lax.broadcasted_iota(jnp.int32, place_ref.shape, 1)
        column = jnp.sum(jnp.where(lanes == expert, place_ref[...], 0.0), axis=1, keepdims=True)
        column_ref[...] = jnp.broadcast_to(column, column_ref.shape)
        total_in_ref[...] = jnp.zeros_like(total_in_ref)
        total_out_ref[...] = jnp.zeros_like(total_out_ref)
        grad_gate_ref[...] = jnp.zeros_like(grad_gate_ref)

    @pl.when(block * ROWS < count_ref[expert])
    def _():
        base = (block * ROWS).astype(jnp.float32)
        row_ids = lax.broadcasted_iota(jnp.int32, (ROWS, tokens), 0).astype(jnp.float32) + base
        hit = row_ids == place_row_ref[0]
        pick = jnp.where(hit, 1.0, 0.0).astype(jnp.bfloat16)
        gate = jnp.sum(jnp.where(hit, gate_row_ref[0], 0.0), axis=1, keepdims=True)
        rows = contract(pick, rows_ref[...], 1, 0).astype(jnp.bfloat16)
        grads = contract(pick, grads_ref[...], 1, 0)
        hidden = contract(rows, in_ref[0], 1, 1)
        square = hidden * hidden
        bend = jnp.tanh(GELU_SCALE * hidden * (1.0 + GELU_CUBE * square))
        active = (0.5 * hidden * (1.0 + bend)).astype(jnp.bfloat16)
        slope = 0.5 * (1.0 + bend) + (0.5 * GELU_SCALE) * hidden * (1.0 - bend * bend) * (
            1.0 + (3.0 * GELU_CUBE) * square
        )
        produced = contract(active, out_ref[0], 1, 0).astype(jnp.bfloat16).astype(jnp.float32)
        grad_produced = (gate * grads).astype(jnp.bfloat16)
        grad_active = contract(grad_produced, out_ref[0], 1, 1)
        grad_hidden = (grad_active * slope).astype(jnp.bfloat16)
        total_in_ref[...] += contract(grad_hidden, rows, 0, 0)
        total_out_ref[...] += contract(active, grad_produced, 0, 0)
        grad_back = contract(grad_hidden, in_ref[0], 1, 0).astype(jnp.bfloat16)
        grad_gate = jnp.sum(grads * produced, axis=1, keepdims=True)
        grad_gate_ref[0] += jnp.sum(jnp.where(hit, grad_gate, 0.0), axis=0, keepdims=True)
        lane_ids = lax.broadcasted_iota(jnp.int32, (tokens, 128), 1).astype(jnp.float32) + base
        column = column_ref[...]
        place = jnp.concatenate(
            [
                jnp.where(column == lane_ids + float(start), 1.0, 0.0).astype(jnp.bfloat16)
                for start in range(0, ROWS, 128)
            ],
            axis=1,
        )
        routed_ref[...] += contract(place, (gate * produced).astype(jnp.bfloat16), 1, 0)
        grad_rows_ref[...] += contract(place, grad_back, 1, 0)

    @pl.when(block == pl.num_programs(1) - 1)
    def _():
        grad_in_ref[0] = total_in_ref[...].astype(jnp.bfloat16)
        grad_out_ref[0] = total_out_ref[...].astype(jnp.bfloat16)


def expert_stage(counts, rows, grads, place_rows, gate_rows, places, full_in, full_out):
    tokens, features = rows.shape
    experts, hidden, _ = full_in.shape
    whole = lambda expert, block, counts: (0, 0)
    single = lambda expert, block, counts: (expert, 0, 0)
    row_spec = pl.BlockSpec((1, 1, tokens), single)
    weight_spec = pl.BlockSpec((1, hidden, features), single)
    token_spec = pl.BlockSpec((tokens, features), whole)
    return pl.pallas_call(
        expert_kernel,
        out_shape=(
            jax.ShapeDtypeStruct((tokens, features), jnp.float32),
            jax.ShapeDtypeStruct((tokens, features), jnp.float32),
            jax.ShapeDtypeStruct((experts, 1, tokens), jnp.float32),
            jax.ShapeDtypeStruct((experts, hidden, features), jnp.bfloat16),
            jax.ShapeDtypeStruct((experts, hidden, features), jnp.bfloat16),
        ),
        grid_spec=pltpu.PrefetchScalarGridSpec(
            num_scalar_prefetch=1,
            grid=(experts, tokens // 2 // ROWS),
            in_specs=[
                token_spec,
                token_spec,
                row_spec,
                row_spec,
                pl.BlockSpec((tokens, experts), whole),
                weight_spec,
                weight_spec,
            ],
            out_specs=[token_spec, token_spec, row_spec, weight_spec, weight_spec],
            scratch_shapes=[
                pltpu.VMEM((tokens, 128), jnp.float32),
                pltpu.VMEM((hidden, features), jnp.float32),
                pltpu.VMEM((hidden, features), jnp.float32),
            ],
        ),
        compiler_params=pltpu.CompilerParams(
            dimension_semantics=("arbitrary", "arbitrary"), vmem_limit_bytes=60 << 20
        ),
        name="expert_stage",
    )(counts, rows, grads, place_rows, gate_rows, places, full_in, full_out)


def place_tokens(routes, first_expert, experts):
    expert_ids = first_expert + jnp.arange(experts, dtype=jnp.int32)
    first_hit = (routes[:, 0:1] == expert_ids[None, :]).astype(jnp.float32)
    second_hit = (routes[:, 1:2] == expert_ids[None, :]).astype(jnp.float32)
    hits = first_hit + second_hit
    chunks = hits.reshape(-1, 256, experts)
    order = jnp.arange(256)
    earlier = (order[:, None] > order[None, :]).astype(jnp.bfloat16)
    within = jnp.einsum(
        "ij,cje->cie", earlier, chunks.astype(jnp.bfloat16), preferred_element_type=jnp.float32
    )
    chunk_totals = jnp.sum(chunks, axis=1)
    chunk_order = jnp.arange(chunks.shape[0])
    chunk_earlier = (chunk_order[:, None] > chunk_order[None, :]).astype(jnp.float32)
    offsets = jnp.sum(chunk_earlier[:, :, None] * chunk_totals[None, :, :], axis=1)
    places = jnp.where(chunks > 0.0, within + offsets[:, None, :], -1.0).reshape(-1, experts)
    counts = jnp.sum(chunk_totals, axis=0).astype(jnp.int32)
    return first_hit, second_hit, places, counts


def split_heads(qkv_block):
    block_count, patches, triple = qkv_block.shape
    features = triple // 3
    head_shape = (block_count, patches, features // HEAD_DIM, HEAD_DIM)
    return (
        qkv_block[..., :features].reshape(head_shape),
        qkv_block[..., features : 2 * features].reshape(head_shape),
        qkv_block[..., 2 * features :].reshape(head_shape),
    )


def attend_forward(qkv_block):
    queries, key_rows, value_rows = split_heads(qkv_block)
    score_scale = HEAD_DIM ** (-0.5)
    scores = (
        jnp.einsum("bqhd,bkhd->bhqk", queries, key_rows, preferred_element_type=jnp.float32)
        * score_scale
    )
    peak_value = jnp.max(scores, axis=-1, keepdims=True)
    shifted = jnp.exp(scores - peak_value)
    denominator = jnp.sum(shifted, axis=-1, keepdims=True)
    probability = (shifted / denominator).astype(jnp.bfloat16)
    mixed_rows = jnp.einsum(
        "bhqk,bkhd->bqhd", probability, value_rows, preferred_element_type=jnp.float32
    )
    mixed_rows = mixed_rows.reshape(qkv_block.shape[0], qkv_block.shape[1], -1).astype(jnp.bfloat16)
    return (mixed_rows, (peak_value + jnp.log(denominator))[..., 0])


def attend_backward(packed):
    qkv_block, grad_mixed, log_total = packed
    queries, key_rows, value_rows = split_heads(qkv_block)
    score_scale = HEAD_DIM ** (-0.5)
    scores = (
        jnp.einsum("bqhd,bkhd->bhqk", queries, key_rows, preferred_element_type=jnp.float32)
        * score_scale
    )
    probability = jnp.exp(scores - log_total[..., None])
    grad_heads = grad_mixed.reshape(queries.shape)
    grad_values = jnp.einsum(
        "bhqk,bqhd->bkhd",
        probability.astype(jnp.bfloat16),
        grad_heads,
        preferred_element_type=jnp.float32,
    )
    grad_probs = jnp.einsum(
        "bqhd,bkhd->bhqk", grad_heads, value_rows, preferred_element_type=jnp.float32
    )
    grad_scores = (
        probability * (grad_probs - jnp.sum(grad_probs * probability, axis=-1, keepdims=True))
    ).astype(jnp.bfloat16)
    grad_queries = (
        jnp.einsum("bhqk,bkhd->bqhd", grad_scores, key_rows, preferred_element_type=jnp.float32)
        * score_scale
    )
    grad_keys = (
        jnp.einsum("bhqk,bqhd->bkhd", grad_scores, queries, preferred_element_type=jnp.float32)
        * score_scale
    )
    merged = jnp.concatenate([grad_queries, grad_keys, grad_values], axis=2)
    return merged.reshape(qkv_block.shape[0], qkv_block.shape[1], -1).astype(jnp.bfloat16)


def spread(block, axis):
    size = lax.axis_size(axis)
    pieces = [block] + [
        lax.ppermute(block, axis, [(source, (source + shift) % size) for source in range(size)])
        for shift in range(1, size)
    ]
    return jnp.concatenate(pieces, axis=0)


def collect(blocks, axis):
    size = lax.axis_size(axis)
    pieces = blocks.reshape(size, -1, blocks.shape[-1])
    total = pieces[0].astype(jnp.float32)
    for shift in range(1, size):
        moved = lax.ppermute(
            pieces[shift], axis, [(source, (source - shift) % size) for source in range(size)]
        )
        total = total + moved.astype(jnp.float32)
    return total


def scatter_halves(blocks, axis, bits):
    size = lax.axis_size(axis)
    index = lax.axis_index(axis)
    experts, hidden, features = blocks.shape
    bit_count = size.bit_length() - 1
    held = blocks.reshape((experts,) + (2,) * bit_count + (hidden // size, features))
    for bit in bits:
        dim = bit_count - bit
        mine = (index >> bit) & 1
        kept = lax.dynamic_slice_in_dim(held, mine, 1, dim)
        sent = lax.dynamic_slice_in_dim(held, 1 - mine, 1, dim)
        moved = lax.ppermute(sent, axis, [(source, source ^ (1 << bit)) for source in range(size)])
        held = (kept.astype(jnp.float32) + moved.astype(jnp.float32)).astype(jnp.bfloat16)
    return held.reshape(experts, hidden // size, features).astype(jnp.float32)


def shards(
    tokens,
    timesteps,
    labels,
    routes,
    time_table,
    class_table,
    ada_weight,
    ada_bias,
    gain_attn,
    gain_ffn,
    qkv_weight,
    proj_weight,
    router_weight,
    shared_in,
    shared_out,
    expert_in,
    expert_out,
    grad_out,
):
    count_tokens, features = tokens.shape
    images = count_tokens // PATCHES
    pair_count = images // 2
    ep_size = lax.axis_size("ep")
    experts = expert_in.shape[0]
    group = lax.axis_index("tg")
    device = group * ep_size + lax.axis_index("ep")
    routes_group = spread(routes, "ep")
    upstream_group = spread(grad_out, "ep")
    full_in = lax.all_gather(expert_in.transpose(0, 2, 1), "tg", axis=1, tiled=True)
    full_out = lax.all_gather(expert_out, "tg", axis=1, tiled=True)
    step_ids = jnp.arange(time_table.shape[0], dtype=jnp.int32)
    class_ids = jnp.arange(class_table.shape[0], dtype=jnp.int32)
    time_hot = (timesteps[:, None] == step_ids[None, :]).astype(jnp.bfloat16)
    class_hot = (labels[:, None] == class_ids[None, :]).astype(jnp.bfloat16)
    condition = jnp.dot(time_hot, time_table, preferred_element_type=jnp.float32) + jnp.dot(
        class_hot, class_table, preferred_element_type=jnp.float32
    )
    silu_low = jax.nn.silu(condition).astype(jnp.bfloat16)
    all_modulation = jnp.dot(silu_low, ada_weight, preferred_element_type=jnp.float32) + ada_bias
    modulation = lax.dynamic_slice_in_dim(all_modulation, device * images, images).reshape(
        images, 6, 1, features
    )
    group_gate = jnp.concatenate(
        [
            lax.dynamic_slice_in_dim(
                all_modulation[:, 5 * features :],
                (group * ep_size + (lax.axis_index("ep") - shift) % ep_size) * images,
                images,
            )
            for shift in range(ep_size)
        ]
    )
    grad_group = (
        (group_gate[:, None, :] * upstream_group.reshape(-1, PATCHES, features))
        .astype(jnp.bfloat16)
        .reshape(-1, features)
    )
    first_hit, second_hit, places, counts = place_tokens(
        routes_group, lax.axis_index("ep") * experts, experts
    )
    residual = tokens.astype(jnp.float32).reshape(images, PATCHES, features)
    normed_attn, inverse_attn = normalize(residual)
    factor_attn = 1.0 + modulation[:, 1]
    attn_in = (
        (normed_attn * gain_attn * factor_attn + modulation[:, 0])
        .astype(jnp.bfloat16)
        .reshape(-1, features)
    )
    qkv_rows = jnp.dot(attn_in, qkv_weight, preferred_element_type=jnp.float32).astype(jnp.bfloat16)
    qkv_blocks = qkv_rows.reshape(pair_count, 2, PATCHES, 3 * features)
    mixed_rows, log_total = lax.map(attend_forward, qkv_blocks)
    mixed_rows = mixed_rows.reshape(-1, features)
    attn_out = jnp.dot(mixed_rows, proj_weight, preferred_element_type=jnp.float32).reshape(
        images, PATCHES, features
    )
    middle = residual + modulation[:, 2] * attn_out
    normed_ffn, inverse_ffn = normalize(middle)
    factor_ffn = 1.0 + modulation[:, 4]
    ffn_in = (
        (normed_ffn * gain_ffn * factor_ffn + modulation[:, 3])
        .astype(jnp.bfloat16)
        .reshape(-1, features)
    )
    rows_group = spread(ffn_in, "ep")
    shared_hidden = jnp.dot(ffn_in, shared_in, preferred_element_type=jnp.float32)
    shared_active = gelu_tanh(shared_hidden).astype(jnp.bfloat16)
    shared_term = jnp.dot(shared_active, shared_out, preferred_element_type=jnp.float32)
    upstream = grad_out.astype(jnp.float32).reshape(images, PATCHES, features)
    grad_ffn = (modulation[:, 5] * upstream).reshape(-1, features)
    grad_shared_low = grad_ffn.astype(jnp.bfloat16)
    grad_shared_out = jnp.einsum(
        "rf,rd->fd", shared_active, grad_shared_low, preferred_element_type=jnp.float32
    )
    grad_shared_active = jnp.einsum(
        "rd,fd->rf", grad_shared_low, shared_out, preferred_element_type=jnp.float32
    )
    grad_shared_hidden = gelu_back(shared_hidden, grad_shared_active).astype(jnp.bfloat16)
    grad_shared_in = jnp.einsum(
        "rd,rf->df", ffn_in, grad_shared_hidden, preferred_element_type=jnp.float32
    )
    grad_ffn_in = jnp.einsum(
        "rf,df->rd", grad_shared_hidden, shared_in, preferred_element_type=jnp.float32
    )
    shared_in_low, shared_out_low, rows_group = lax.optimization_barrier(
        (grad_shared_in.astype(jnp.bfloat16), grad_shared_out.astype(jnp.bfloat16), rows_group)
    )
    shared_in_sum, shared_out_sum = lax.psum((shared_in_low, shared_out_low), ("tg", "ep"))
    route_ids = jnp.arange(router_weight.shape[1], dtype=jnp.int32)
    first_hot = (routes_group[:, 0:1] == route_ids[None, :]).astype(jnp.float32)
    second_hot = (routes_group[:, 1:2] == route_ids[None, :]).astype(jnp.float32)
    logits = jnp.dot(rows_group, router_weight, preferred_element_type=jnp.float32)
    first_logit = jnp.sum(logits * first_hot, axis=1, keepdims=True)
    second_logit = jnp.sum(logits * second_hot, axis=1, keepdims=True)
    peak_logit = jnp.maximum(first_logit, second_logit)
    first_power = jnp.exp(first_logit - peak_logit)
    second_power = jnp.exp(second_logit - peak_logit)
    first_gate = first_power / (first_power + second_power)
    second_gate = second_power / (first_power + second_power)
    gates_here = first_hit * first_gate + second_hit * second_gate
    routed_part, grad_rows_part, grad_gates, grad_in_part, grad_out_part = expert_stage(
        counts,
        rows_group,
        grad_group,
        places.T[:, None, :],
        gates_here.T[:, None, :],
        places,
        full_in,
        full_out,
    )
    grad_hits = grad_gates[:, 0, :].T
    gate_pull = (
        first_gate
        * second_gate
        * jnp.sum(grad_hits * (first_hit - second_hit), axis=1, keepdims=True)
    )
    grad_logits = gate_pull * (first_hot - second_hot)
    grad_router = jnp.einsum(
        "rd,re->de",
        rows_group.astype(jnp.float32),
        grad_logits,
        precision=lax.Precision.HIGHEST,
    )
    grad_rows_part = grad_rows_part + jnp.einsum(
        "re,de->rd", grad_logits, router_weight.astype(jnp.float32), precision=lax.Precision.HIGHEST
    )
    grad_ffn_in = grad_ffn_in + collect(grad_rows_part.astype(jnp.bfloat16), "ep")
    grad_ffn_in, routed_low = lax.optimization_barrier(
        (grad_ffn_in, routed_part.astype(jnp.bfloat16))
    )
    routed = collect(routed_low, "ep")
    ffn_out = (routed + shared_term).reshape(images, PATCHES, features)
    output = (middle + modulation[:, 5] * ffn_out).reshape(-1, features).astype(jnp.bfloat16)
    grad_gate_ffn = jnp.sum(upstream * ffn_out, axis=1)
    tg_bits = lax.axis_size("tg").bit_length() - 1
    near_bits = list(range(1, 1 + (tg_bits - 1) // 2))
    far_bits = list(range(1 + (tg_bits - 1) // 2, tg_bits))
    shard_in = scatter_halves(grad_in_part, "tg", [0] + near_bits + far_bits).transpose(0, 2, 1)
    shard_out = scatter_halves(grad_out_part, "tg", [0] + far_bits + near_bits)
    grad_ffn_cube = grad_ffn_in.reshape(images, PATCHES, features)
    grad_shift_ffn = jnp.sum(grad_ffn_cube, axis=1)
    cross_ffn = jnp.sum(grad_ffn_cube * normed_ffn, axis=1)
    grad_middle = upstream + norm_back(
        grad_ffn_cube * gain_ffn * factor_ffn, normed_ffn, inverse_ffn
    )
    grad_gate_attn = jnp.sum(grad_middle * attn_out, axis=1)
    grad_attn_low = (modulation[:, 2] * grad_middle).reshape(-1, features).astype(jnp.bfloat16)
    grad_proj = jnp.einsum(
        "rd,re->de", mixed_rows, grad_attn_low, preferred_element_type=jnp.float32
    )
    grad_mixed = jnp.einsum(
        "re,de->rd", grad_attn_low, proj_weight, preferred_element_type=jnp.float32
    ).astype(jnp.bfloat16)
    grad_qkv = lax.map(
        attend_backward,
        (qkv_blocks, grad_mixed.reshape(pair_count, 2, PATCHES, features), log_total),
    ).reshape(-1, 3 * features)
    grad_qkv_weight = jnp.einsum("rd,re->de", attn_in, grad_qkv, preferred_element_type=jnp.float32)
    grad_attn_in = jnp.einsum(
        "re,de->rd", grad_qkv, qkv_weight, preferred_element_type=jnp.float32
    ).reshape(images, PATCHES, features)
    grad_shift_attn = jnp.sum(grad_attn_in, axis=1)
    cross_attn = jnp.sum(grad_attn_in * normed_attn, axis=1)
    grad_tokens = grad_middle + norm_back(
        grad_attn_in * gain_attn * factor_attn, normed_attn, inverse_attn
    )
    grad_qkv_weight, shared_in_sum, shared_out_sum = lax.optimization_barrier(
        (grad_qkv_weight, shared_in_sum, shared_out_sum)
    )
    local_sums = jnp.concatenate(
        [grad_shift_attn, cross_attn, grad_gate_attn, grad_shift_ffn, cross_ffn, grad_gate_ffn],
        axis=1,
    )
    image_owner = jnp.arange(timesteps.shape[0]) // images == device
    placed_sums = jnp.where(
        image_owner[:, None], jnp.tile(local_sums, (timesteps.shape[0] // images, 1)), 0.0
    )
    stacked_grads = jnp.concatenate([grad_proj, grad_router.T], axis=0)
    image_sums, qkv_sum, stacked_sum = (
        item.astype(jnp.float32)
        for item in lax.psum(
            tuple(
                item.astype(jnp.bfloat16)
                for item in (placed_sums, grad_qkv_weight, stacked_grads)
            ),
            ("tg", "ep"),
        )
    )
    image_sums = image_sums.reshape(-1, 6, features)
    proj_sum, router_sum = stacked_sum[:features], stacked_sum[features:].T
    all_pieces = all_modulation.reshape(-1, 6, features)
    grad_gain_attn = jnp.sum(image_sums[:, 1] * (1.0 + all_pieces[:, 1]), axis=0)
    grad_gain_ffn = jnp.sum(image_sums[:, 4] * (1.0 + all_pieces[:, 4]), axis=0)
    ones = jnp.ones_like(gain_attn)
    piece_gains = jnp.stack([ones, gain_attn, ones, ones, gain_ffn, ones])
    grad_modulation = (image_sums * piece_gains).reshape(-1, 6 * features)
    grad_ada_bias = jnp.sum(grad_modulation, axis=0)
    grad_ada_weight = jnp.einsum(
        "id,ie->de", silu_low.astype(jnp.float32), grad_modulation, precision=lax.Precision.HIGHEST
    )
    grad_silu = jnp.einsum(
        "ie,de->id",
        grad_modulation,
        ada_weight.astype(jnp.float32),
        precision=lax.Precision.HIGHEST,
    )
    grad_condition = jax.vjp(jax.nn.silu, condition)[1](grad_silu)[0]
    time_term = jnp.einsum(
        "is,id->sd", time_hot.astype(jnp.float32), grad_condition, precision=lax.Precision.HIGHEST
    )
    class_term = jnp.einsum(
        "ic,id->cd", class_hot.astype(jnp.float32), grad_condition, precision=lax.Precision.HIGHEST
    )
    return (
        output,
        grad_tokens.reshape(-1, features),
        time_term,
        class_term,
        grad_ada_weight,
        grad_ada_bias,
        grad_gain_attn,
        grad_gain_ffn,
        qkv_sum,
        proj_sum,
        router_sum,
        shared_in_sum.astype(jnp.float32),
        shared_out_sum.astype(jnp.float32),
        shard_in,
        shard_out,
    )


def solution(mesh):
    in_specs = (
        P(("tg", "ep"), None),
        P(),
        P(),
        P(("tg", "ep"), None),
        P(),
        P(),
        P(),
        P(),
        P(),
        P(),
        P(),
        P(),
        P(),
        P(),
        P(),
        P("ep", None, "tg"),
        P("ep", "tg", None),
        P(("tg", "ep"), None),
    )
    out_specs = (
        P(("tg", "ep"), None),
        P(("tg", "ep"), None),
        P(),
        P(),
        P(),
        P(),
        P(),
        P(),
        P(),
        P(),
        P(),
        P(),
        P(),
        P("ep", None, "tg"),
        P("ep", "tg", None),
    )
    return jax.shard_map(shards, mesh=mesh, in_specs=in_specs, out_specs=out_specs, check_vma=False)
```
